32 devices in a mesh: parts: 2 (over x), blk: 16 (over z, y, core).
Axes of the slice: x: 2, y: 2, z: 4, core: 2. Of those that a mesh axis runs over, the one named last changes fastest.
Arguments:
- observed: bfloat16 [24576, 1024], P(('parts', 'blk')), parts along dimension 0, may hold values from -6 to 6
- sharpness: float32 [24576], P(('parts', 'blk')), parts along dimension 0, may hold values from 0.03 to 0.15
- obs_class: int32 [24576], P(('parts', 'blk')), parts along dimension 0, may hold values from 0 to 7
- pattern: int32 [192, 16], P(('parts', 'blk')), parts along dimension 0, may hold values from 0 to 1, as said below
- evolved: bfloat16 [4096, 1024], P(('parts', 'blk')), parts along dimension 0, may hold values from -6 to 6
- sim_params: bfloat16 [4, 4096], P(None, ('parts', 'blk')), parts along dimension 1, may hold values from -6 to 6
- sim_class: int32 [4096], P(('parts', 'blk')), parts along dimension 0, may hold values from 0 to 7, as said below
Outputs:
- posterior_mean: float32 [4, 24576], P(None, ('parts', 'blk')), parts along dimension 1
- log_evidence: float32 [24576], P(('parts', 'blk')), parts along dimension 0
The draws below stay inside these ranges and needn't reach their ends.
There are 2 independent parts, one for each index of `parts`. The reference program is written for one: setup_inputs(seed, part) draws one part's arguments, and reference() takes and returns one part's arrays. A program takes and returns all parts, laid end to end along the dimension named above; each array names one. Nothing has to cross between parts.
Inputs may be any that keep to these rules, and one draw needn't show every extreme that they name: `sim_class`: every block of 128 evolved profiles holds every class, at its first 8 positions. `pattern`: every block of observed profiles is compared with at least one block of evolved profiles; the share of compared blocks differs from one observed block to another.
All inputs are finite; a program needn't handle non-finite values.
Results may differ from the reference program's by a relative error of at most 0.0045.
Values may be sent and summed in bfloat16 or wider, within the bound.
A program may use at most 64 MiB of HBM per device.

```python
import math
import jax
import jax.numpy as jnp
from jax import lax

P_SIZE = 1024
NPARAM = 4
NCLASS = 8
BLOCK = 128
NOBS = 12288
NSIM = 2048
OBS_BLOCKS = 96
SIM_BLOCKS = 16


def class_tables(key):
    key_sim = jax.random.fold_in(key, 101)
    key_obs = jax.random.fold_in(key, 102)
    key_level = jax.random.fold_in(key, 103)
    key_mask = jax.random.fold_in(key, 104)
    key_force = jax.random.fold_in(key, 105)
    sim_class = jax.random.randint(key_sim, (NSIM,), 0, NCLASS)
    within = jnp.arange(NSIM) % BLOCK
    sim_class = jnp.where(within < NCLASS, within, sim_class).astype(jnp.int32)
    obs_class = jax.random.randint(key_obs, (NOBS,), 0, NCLASS).astype(jnp.int32)
    levels = jax.random.randint(key_level, (OBS_BLOCKS, 1), 1, 9)
    rolls = jax.random.randint(key_mask, (OBS_BLOCKS, SIM_BLOCKS), 0, 16)
    forced = jax.random.randint(key_force, (OBS_BLOCKS, 1), 0, SIM_BLOCKS)
    opened = (rolls < levels) | (jnp.arange(SIM_BLOCKS)[None, :] == forced)
    return (obs_class, sim_class, opened.astype(jnp.int32))


def sim_values(key):
    key_base = jax.random.fold_in(key, 201)
    base = jax.random.normal(key_base, (NSIM, P_SIZE), jnp.float32)
    return jnp.clip(base, -6.0, 6.0)


def draw_obs_class(key, part):
    return class_tables(key)[0]


def draw_sim_class(key, part):
    return class_tables(key)[1]


def draw_pattern(key, part):
    return class_tables(key)[2]


def draw_evolved(key, part):
    return sim_values(key).astype(jnp.bfloat16)


def draw_observed(key, part):
    key_own = jax.random.fold_in(key, 301)
    base = jax.random.normal(key_own, (NOBS, P_SIZE), jnp.float32)
    return jnp.clip(base, -6.0, 6.0).astype(jnp.bfloat16)


def block_levels(rng, shape, shards, least, largest):
    factor_of = 1.0
    for dim, blocks in shards:
        draws = jax.random.uniform(jax.random.fold_in(jax.random.fold_in(rng, 6), dim), (blocks,), jnp.float32, least / len(shards), largest / len(shards))
        factor_of = factor_of * jnp.repeat(jnp.exp(draws), shape[dim] // blocks).reshape((-1,) + (1,) * (len(shape) - 1 - dim))
    return factor_of


def gaussian(key, dims, spread, limit, shards=(), held_as=jnp.bfloat16):
    gain = block_levels(key, dims, shards, -0.22, 0.18) if shards else 1.0
    array = jax.random.normal(key, dims, jnp.float32) * spread * gain
    return jnp.minimum(jnp.maximum(array, -limit), limit).astype(held_as)


def setup_inputs(seed: int = 0, part: int = 0) -> dict:
    splits = jax.random.split(jax.random.key(seed), 8)
    part_keys = jax.random.split(jax.random.fold_in(splits[7], part), 8)
    observed = draw_observed(jax.random.fold_in(jax.random.fold_in(splits[7], part), 71), part)
    sharpness = jnp.clip(jnp.exp(math.log(0.15) - 1.609438 * jax.random.uniform(part_keys[1], (NOBS,), jnp.float32) ** block_levels(part_keys[1], (NOBS,), ((0, 16),), -0.2, 0.2)), 0.03, 0.15)
    obs_class = draw_obs_class(jax.random.fold_in(jax.random.fold_in(splits[7], part), 71), part)
    pattern = draw_pattern(jax.random.fold_in(jax.random.fold_in(splits[7], part), 71), part)
    evolved = draw_evolved(jax.random.fold_in(jax.random.fold_in(splits[7], part), 71), part)
    sim_params = gaussian(part_keys[5], (NPARAM, NSIM), 1.0, 6.0, ((1, 16),))
    sim_class = draw_sim_class(jax.random.fold_in(jax.random.fold_in(splits[7], part), 71), part)
    return dict(observed=observed, sharpness=sharpness, obs_class=obs_class, pattern=pattern, evolved=evolved, sim_params=sim_params, sim_class=sim_class)


NEG_START = -1.0e30


def visit_block(observed, obs_sq, sharpness, obs_class, rows_open, sims, params, sims_class, running_max, weight_total, param_sums):
    sims_sq = jnp.sum(jnp.square(sims.astype(jnp.float32)), axis=1)
    inner = lax.dot_general(observed, sims, (((1,), (1,)), ((), ())), preferred_element_type=jnp.float32)
    distance = obs_sq[:, None] + sims_sq[None, :] - 2.0 * inner
    score = sharpness[:, None] * (2.0 * P_SIZE - distance)
    active = rows_open[:, None] & (obs_class[:, None] == sims_class[None, :])
    new_max = jnp.maximum(running_max, jnp.max(jnp.where(active, score, NEG_START), axis=1))
    factor = jnp.exp(running_max - new_max)
    weights = jnp.where(active, jnp.exp(score - new_max[:, None]), 0.0)
    weight_total = weight_total * factor + jnp.sum(weights, axis=1)
    weight_low = weights.astype(jnp.bfloat16)
    added = lax.dot_general(params, weight_low, (((1,), (1,)), ((), ())), preferred_element_type=jnp.float32)
    param_sums = param_sums * factor[None, :] + added
    return new_max, weight_total, param_sums


def reference(observed, sharpness, obs_class, pattern, evolved, sim_params, sim_class):
    obs_sq = jnp.sum(jnp.square(observed.astype(jnp.float32)), axis=1)
    row_block = (jnp.arange(NOBS) // BLOCK).astype(jnp.int32)
    sims_all = evolved.reshape(SIM_BLOCKS, BLOCK, P_SIZE)
    params_all = jnp.transpose(sim_params.reshape(NPARAM, SIM_BLOCKS, BLOCK), (1, 0, 2))
    class_all = sim_class.reshape(SIM_BLOCKS, BLOCK)
    block_ids = jnp.arange(SIM_BLOCKS).astype(jnp.int32)

    def step(carry, inputs):
        sims, params, sims_class, block_id = inputs
        column = lax.dynamic_slice_in_dim(pattern, block_id, 1, 1)[:, 0]
        rows_open = column[row_block] == 1
        result = visit_block(observed, obs_sq, sharpness, obs_class, rows_open, sims, params, sims_class, carry[0], carry[1], carry[2])
        return result, None

    start = (jnp.full((NOBS,), NEG_START, jnp.float32), jnp.zeros((NOBS,), jnp.float32), jnp.zeros((NPARAM, NOBS), jnp.float32))
    final, _ = lax.scan(step, start, (sims_all, params_all, class_all, block_ids))
    running_max, weight_total, param_sums = final
    return param_sums / weight_total[None, :], running_max + jnp.log(weight_total)
```

```python
import functools

import jax
import jax.numpy as jnp
from jax import lax
from jax.experimental import pallas as pl
from jax.experimental.pallas import tpu as pltpu
from jax.sharding import PartitionSpec as P

NEG_START = -1e30
NEG_MASK = -3e38
LANES = 128
AUX_ROWS = 16
MESH = pl.DeviceIdType.MESH


def kernel(
    depth,
    obs_hbm,
    sharp_ref,
    ocls_ref,
    pat_ref,
    evo_hbm,
    prm_ref,
    scls_ref,
    mean_ref,
    lev_ref,
    gat,
    obs,
    evo,
    stage,
    base_sc,
    max_sc,
    tot_sc,
    sum_sc,
    local_sem,
    up_send,
    dn_send,
    y_send,
    s_send,
    z_recv,
    y_recv,
    s_recv,
):
    me = lax.axis_index("blk")
    z, y, c = me // 4, (me // 2) % 2, me % 2
    rows, feat = obs.shape
    sims = evo.shape[0]
    tiles = feat // LANES
    tile_count = pat_ref.shape[0]
    tile_rows = rows // tile_count
    nparam = prm_ref.shape[0]

    def blk_of(zz, yy, cc):
        return zz * 4 + yy * 2 + cc

    evo_copy = pltpu.make_async_copy(evo_hbm, evo, local_sem.at[0])
    obs_copy = pltpu.make_async_copy(obs_hbm, obs, local_sem.at[1])
    evo_copy.start()
    obs_copy.start()

    has_up = z < depth - 1
    has_dn = z > 0

    barrier = pltpu.get_barrier_semaphore()

    def greet(dev):
        pl.semaphore_signal(barrier, inc=1, device_id={"blk": dev}, device_id_type=MESH)

    greet(blk_of(z, y, 1 - c))
    greet(blk_of(z, 1 - y, c))

    @pl.when(has_up)
    def _():
        greet(blk_of(z + 1, y, c))

    @pl.when(has_dn)
    def _():
        greet(blk_of(z - 1, y, c))

    stage[...] = jnp.zeros_like(stage)
    stage[0:nparam, :] = prm_ref[...].astype(jnp.float32)
    stage[nparam : nparam + 1, :] = scls_ref[...].astype(jnp.float32)
    evo_copy.wait()
    for t in range(tiles):
        gat[z, y, c, t * sims : (t + 1) * sims, :] = evo[:, t * LANES : (t + 1) * LANES]
    gat[z, y, c, tiles * sims : tiles * sims + AUX_ROWS, :] = stage[...].astype(jnp.bfloat16)

    peers = 2 + (z + depth - 1) // depth + (2 * depth - 2 - z) // depth
    pl.semaphore_wait(barrier, peers)

    def packet(o, yy, cc, dev, send, recv):
        return pltpu.make_async_remote_copy(
            src_ref=gat.at[o, yy, cc],
            dst_ref=gat.at[o, yy, cc],
            send_sem=send,
            recv_sem=recv,
            device_id={"blk": dev},
            device_id_type=MESH,
        )

    def to_up(o):
        return packet(o, y, c, blk_of(z + 1, y, c), up_send.at[o], z_recv.at[o])

    def to_dn(o):
        return packet(o, y, c, blk_of(z - 1, y, c), dn_send.at[o], z_recv.at[o])

    def to_y(o):
        return packet(o, y, c, blk_of(z, 1 - y, c), y_send.at[o], y_recv.at[o])

    def from_y(o):
        return packet(o, 1 - y, c, blk_of(z, 1 - y, c), y_send.at[o], y_recv.at[o])

    def to_core(o, yy):
        return packet(
            o, yy, c, blk_of(z, y, 1 - c), s_send.at[o * 2 + yy], s_recv.at[o * 2 + yy]
        )

    def from_core(o, yy):
        return packet(
            o, yy, 1 - c, blk_of(z, y, 1 - c), s_send.at[o * 2 + yy], s_recv.at[o * 2 + yy]
        )

    @pl.when(has_up)
    def _():
        to_up(z).start()

    @pl.when(has_dn)
    def _():
        to_dn(z).start()

    to_y(z).start()
    to_core(z, y).start()

    obs_copy.wait()
    for i in range(rows // LANES):
        part = obs[i * LANES : (i + 1) * LANES, :].astype(jnp.float32)
        col = jnp.sum(part * part, axis=1, keepdims=True)
        wide = jnp.broadcast_to(col, (LANES, LANES)).T
        base_sc[0:1, i * LANES : (i + 1) * LANES] = 1.0 * feat - 0.5 * wide[0:1, :]

    max_sc[...] = jnp.full_like(max_sc, NEG_START)
    tot_sc[...] = jnp.zeros_like(tot_sc)
    sum_sc[...] = jnp.zeros_like(sum_sc)
    group = 2 if tile_count % 2 == 0 else 1
    width = group * tile_rows

    def absorb(o, yy):
        lhs, half_sq, classes, aux = [], [], [], []
        for cc in range(2):
            block = jnp.concatenate(
                [gat[o, yy, cc, t * sims : (t + 1) * sims, :] for t in range(tiles)], axis=1
            )
            wide = block.astype(jnp.float32)
            half_sq.append(0.5 * jnp.sum(wide * wide, axis=1, keepdims=True))
            extra = gat[o, yy, cc, tiles * sims : tiles * sims + AUX_ROWS, :]
            row = extra.astype(jnp.float32)[nparam : nparam + 1, :]
            turned = jnp.broadcast_to(row, (LANES, LANES)).T
            classes.append(turned[:, 0:1])
            aux.append(extra)
            lhs.append(block)
        lhs = jnp.concatenate(lhs, axis=0)
        for g in range(tile_count // group):
            span = slice(g * width, (g + 1) * width)
            inner = lax.dot_general(
                lhs, obs[span, :], (((1,), (1,)), ((), ())), preferred_element_type=jnp.float32
            )
            sharp2 = 2.0 * sharp_ref[0:1, span]
            base = base_sc[0:1, span]
            masked = []
            for cc in range(2):
                wanted = jnp.concatenate(
                    [
                        jnp.where(
                            pat_ref[i, blk_of(o, yy, cc)] == 1,
                            ocls_ref[0:1, i * tile_rows : (i + 1) * tile_rows],
                            -1,
                        )
                        for i in range(g * group, (g + 1) * group)
                    ],
                    axis=1,
                ).astype(jnp.float32)
                score = ((inner[cc * sims : (cc + 1) * sims] - half_sq[cc]) + base) * sharp2
                masked.append(jnp.where(classes[cc] == wanted, score, NEG_MASK))
            top = jnp.max(jnp.maximum(masked[0], masked[1]), axis=0, keepdims=True)
            old = max_sc[0:1, span]
            new = jnp.maximum(old, top)
            factor = jnp.exp(old - new)
            w0 = jnp.exp(masked[0] - new)
            w1 = jnp.exp(masked[1] - new)
            max_sc[0:1, span] = new
            tot_sc[0:1, span] = tot_sc[0:1, span] * factor + jnp.sum(
                w0 + w1, axis=0, keepdims=True
            )
            added = lax.dot_general(
                jnp.concatenate(aux, axis=1),
                jnp.concatenate([w0, w1], axis=0).astype(jnp.bfloat16),
                (((1,), (0,)), ((), ())),
                preferred_element_type=jnp.float32,
            )
            sum_sc[:, span] = sum_sc[:, span] * factor + added

    def step(s, carry):
        lo, hi = z - s, z + s
        has_lo, has_hi = lo >= 0, hi < depth
        lo_y, hi_y = z - s + 1, z + s - 1
        has_lo_y = lo_y >= 0
        has_hi_y = (hi_y < depth) & (s > 1)

        @pl.when(has_lo)
        def _():
            to_up(lo).wait_recv()

            @pl.when(has_up)
            def _():
                to_up(lo).start()

            to_y(lo).start()
            to_core(lo, y).start()

        @pl.when(has_hi & (s > 0))
        def _():
            to_dn(hi).wait_recv()

            @pl.when(has_dn)
            def _():
                to_dn(hi).start()

            to_y(hi).start()
            to_core(hi, y).start()

        @pl.when(has_lo_y)
        def _():
            from_y(lo_y).wait_recv()
            to_core(lo_y, 1 - y).start()

        @pl.when(has_hi_y)
        def _():
            from_y(hi_y).wait_recv()
            to_core(hi_y, 1 - y).start()

        def take(q, carry_q):
            side, late = q % 2, q // 2
            dist = s - late
            o = z + (2 * side - 1) * dist
            yy = y + late * (1 - 2 * y)

            @pl.when((o >= 0) & (o < depth) & ((dist > 0) | (side == 0)))
            def _():
                from_core(o, yy).wait_recv()
                absorb(o, yy)

            return carry_q

        return lax.fori_loop(0, 4, take, carry)

    from_core(z, y).wait_recv()
    absorb(z, y)
    lax.fori_loop(1, depth + 1, step, 0)

    def drain(o, carry):
        to_y(o).wait_send()
        to_core(o, 0).wait_send()
        to_core(o, 1).wait_send()

        @pl.when(has_up & (o <= z))
        def _():
            to_up(o).wait_send()

        @pl.when(has_dn & (o >= z))
        def _():
            to_dn(o).wait_send()

        return carry

    lax.fori_loop(0, depth, drain, 0)

    total = tot_sc[...]
    mean_ref[...] = sum_sc[0:nparam, :] / total
    lev_ref[...] = max_sc[...] + jnp.log(total)


def solution(mesh):
    depth = mesh.shape["blk"] // 4

    def on_device(observed, sharpness, obs_class, pattern, evolved, sim_params, sim_class):
        rows, feat = observed.shape
        sims = evolved.shape[0]
        nparam = sim_params.shape[0]
        packet_rows = feat // LANES * sims + AUX_ROWS
        vmem = pl.BlockSpec(memory_space=pltpu.VMEM)
        hbm = pl.BlockSpec(memory_space=pltpu.HBM)
        dma = pltpu.SemaphoreType.DMA
        mean, lev = pl.pallas_call(
            functools.partial(kernel, depth),
            out_shape=(
                jax.ShapeDtypeStruct((nparam, rows), jnp.float32),
                jax.ShapeDtypeStruct((1, rows), jnp.float32),
            ),
            in_specs=[hbm, vmem, vmem, pl.BlockSpec(memory_space=pltpu.SMEM), hbm, vmem, vmem],
            out_specs=(vmem, vmem),
            scratch_shapes=[
                pltpu.VMEM((depth, 2, 2, packet_rows, LANES), jnp.bfloat16),
                pltpu.VMEM((rows, feat), jnp.bfloat16),
                pltpu.VMEM((sims, feat), jnp.bfloat16),
                pltpu.VMEM((AUX_ROWS, LANES), jnp.float32),
                pltpu.VMEM((1, rows), jnp.float32),
                pltpu.VMEM((1, rows), jnp.float32),
                pltpu.VMEM((1, rows), jnp.float32),
                pltpu.VMEM((AUX_ROWS, rows), jnp.float32),
                dma((2,)),
                dma((depth,)),
                dma((depth,)),
                dma((depth,)),
                dma((2 * depth,)),
                dma((depth,)),
                dma((depth,)),
                dma((2 * depth,)),
            ],
            compiler_params=pltpu.CompilerParams(
                collective_id=0, has_side_effects=True, vmem_limit_bytes=40 << 20
            ),
        )(
            observed,
            sharpness.reshape(1, rows),
            obs_class.reshape(1, rows),
            pattern,
            evolved,
            sim_params,
            sim_class.reshape(1, sims),
        )
        return mean, lev.reshape(rows)

    placed = (
        P(("parts", "blk"), None),
        P(("parts", "blk")),
        P(("parts", "blk")),
        P(("parts", "blk"), None),
        P(("parts", "blk"), None),
        P(None, ("parts", "blk")),
        P(("parts", "blk")),
    )
    return jax.shard_map(
        on_device,
        mesh=mesh,
        in_specs=placed,
        out_specs=(P(None, ("parts", "blk")), P(("parts", "blk"))),
        check_vma=False,
    )
```

```python
import functools

import jax
import jax.numpy as jnp
from jax import lax
from jax.experimental import pallas as pl
from jax.experimental.pallas import tpu as pltpu
from jax.sharding import PartitionSpec as P

NEG_START = -1e30
NEG_MASK = -3e38
LANES = 128
AUX_ROWS = 16
MESH = pl.DeviceIdType.MESH


def kernel(
    depth,
    obs_hbm,
    sharp_hbm,
    ocls_hbm,
    pat_hbm,
    evo_hbm,
    prm_hbm,
    scls_hbm,
    mean_ref,
    lev_ref,
    gat,
    obs,
    evo,
    sharp_in,
    ocls_in,
    pat_ref,
    prm_ref,
    scls_in,
    stage,
    sharp_ref,
    ocls_ref,
    base_sc,
    max_sc,
    tot_sc,
    sum_sc,
    local_sem,
    up_send,
    dn_send,
    y_send,
    s_send,
    z_recv,
    y_recv,
    s_recv,
):
    me = lax.axis_index("blk")
    z, y, c = me // 4, (me // 2) % 2, me % 2
    rows, feat = obs.shape
    sims = evo.shape[0]
    tiles = feat // LANES
    tile_count = pat_hbm.shape[0]
    tile_rows = rows // tile_count
    nparam = prm_hbm.shape[0]

    def blk_of(zz, yy, cc):
        return zz * 4 + yy * 2 + cc

    evo_copy = pltpu.make_async_copy(evo_hbm, evo, local_sem.at[0])
    prm_copy = pltpu.make_async_copy(prm_hbm, prm_ref, local_sem.at[1])
    scls_copy = pltpu.make_async_copy(scls_hbm, scls_in, local_sem.at[2])
    obs_copy = pltpu.make_async_copy(obs_hbm, obs, local_sem.at[3])
    sharp_copy = pltpu.make_async_copy(sharp_hbm, sharp_in, local_sem.at[4])
    ocls_copy = pltpu.make_async_copy(ocls_hbm, ocls_in, local_sem.at[5])
    pat_copy = pltpu.make_async_copy(pat_hbm, pat_ref, local_sem.at[6])
    for copy in (evo_copy, prm_copy, scls_copy, obs_copy, sharp_copy, ocls_copy, pat_copy):
        copy.start()

    has_up = z < depth - 1
    has_dn = z > 0

    barrier = pltpu.get_barrier_semaphore()

    def greet(dev):
        pl.semaphore_signal(barrier, inc=1, device_id={"blk": dev}, device_id_type=MESH)

    greet(blk_of(z, y, 1 - c))
    greet(blk_of(z, 1 - y, c))

    @pl.when(has_up)
    def _():
        greet(blk_of(z + 1, y, c))

    @pl.when(has_dn)
    def _():
        greet(blk_of(z - 1, y, c))

    stage[...] = jnp.zeros_like(stage)
    prm_copy.wait()
    stage[0:nparam, :] = prm_ref[...].astype(jnp.float32)
    scls_copy.wait()
    stage[nparam : nparam + 1, :] = scls_in[...].reshape(1, sims).astype(jnp.float32)
    evo_copy.wait()
    for t in range(tiles):
        gat[z, y, c, t * sims : (t + 1) * sims, :] = evo[:, t * LANES : (t + 1) * LANES]
    gat[z, y, c, tiles * sims : tiles * sims + AUX_ROWS, :] = stage[...].astype(jnp.bfloat16)

    peers = 2 + (z + depth - 1) // depth + (2 * depth - 2 - z) // depth
    pl.semaphore_wait(barrier, peers)

    def packet(o, yy, cc, dev, send, recv):
        return pltpu.make_async_remote_copy(
            src_ref=gat.at[o, yy, cc],
            dst_ref=gat.at[o, yy, cc],
            send_sem=send,
            recv_sem=recv,
            device_id={"blk": dev},
            device_id_type=MESH,
        )

    def to_up(o):
        return packet(o, y, c, blk_of(z + 1, y, c), up_send.at[o], z_recv.at[o])

    def to_dn(o):
        return packet(o, y, c, blk_of(z - 1, y, c), dn_send.at[o], z_recv.at[o])

    def to_y(o):
        return packet(o, y, c, blk_of(z, 1 - y, c), y_send.at[o], y_recv.at[o])

    def from_y(o):
        return packet(o, 1 - y, c, blk_of(z, 1 - y, c), y_send.at[o], y_recv.at[o])

    def to_core(o, yy):
        return packet(
            o, yy, c, blk_of(z, y, 1 - c), s_send.at[o * 2 + yy], s_recv.at[o * 2 + yy]
        )

    def from_core(o, yy):
        return packet(
            o, yy, 1 - c, blk_of(z, y, 1 - c), s_send.at[o * 2 + yy], s_recv.at[o * 2 + yy]
        )

    @pl.when(has_up)
    def _():
        to_up(z).start()

    @pl.when(has_dn)
    def _():
        to_dn(z).start()

    to_y(z).start()
    to_core(z, y).start()

    sharp_copy.wait()
    ocls_copy.wait()
    pat_copy.wait()
    obs_copy.wait()
    for i in range(rows // LANES):
        lanes = slice(i * LANES, (i + 1) * LANES)
        sharp_ref[0:1, lanes] = 2.0 * sharp_in[lanes].reshape(1, LANES)
        ocls_ref[0:1, lanes] = ocls_in[lanes].reshape(1, LANES)
        part = obs[i * LANES : (i + 1) * LANES, :].astype(jnp.float32)
        col = jnp.sum(part * part, axis=1, keepdims=True)
        wide = jnp.broadcast_to(col, (LANES, LANES)).T
        base_sc[0:1, i * LANES : (i + 1) * LANES] = 1.0 * feat - 0.5 * wide[0:1, :]

    max_sc[...] = jnp.full_like(max_sc, NEG_START)
    tot_sc[...] = jnp.zeros_like(tot_sc)
    sum_sc[...] = jnp.zeros_like(sum_sc)
    group = 2 if tile_count % 2 == 0 else 1
    width = group * tile_rows

    def absorb(o, yy):
        lhs, half_sq, classes, aux = [], [], [], []
        for cc in range(2):
            block = jnp.concatenate(
                [gat[o, yy, cc, t * sims : (t + 1) * sims, :] for t in range(tiles)], axis=1
            )
            wide = block.astype(jnp.float32)
            half_sq.append(0.5 * jnp.sum(wide * wide, axis=1, keepdims=True))
            extra = gat[o, yy, cc, tiles * sims : tiles * sims + AUX_ROWS, :]
            row = extra.astype(jnp.float32)[nparam : nparam + 1, :]
            turned = jnp.broadcast_to(row, (LANES, LANES)).T
            classes.append(turned[:, 0:1])
            aux.append(extra)
            lhs.append(block)
        lhs = jnp.concatenate(lhs, axis=0)
        for g in range(tile_count // group):
            span = slice(g * width, (g + 1) * width)
            inner = lax.dot_general(
                lhs, obs[span, :], (((1,), (1,)), ((), ())), preferred_element_type=jnp.float32
            )
            sharp2 = sharp_ref[0:1, span]
            base = base_sc[0:1, span]
            masked = []
            for cc in range(2):
                wanted = jnp.concatenate(
                    [
                        jnp.where(
                            pat_ref[i, blk_of(o, yy, cc)] == 1,
                            ocls_ref[0:1, i * tile_rows : (i + 1) * tile_rows],
                            -1,
                        )
                        for i in range(g * group, (g + 1) * group)
                    ],
                    axis=1,
                ).astype(jnp.float32)
                score = ((inner[cc * sims : (cc + 1) * sims] - half_sq[cc]) + base) * sharp2
                masked.append(jnp.where(classes[cc] == wanted, score, NEG_MASK))
            top = jnp.max(jnp.maximum(masked[0], masked[1]), axis=0, keepdims=True)
            old = max_sc[0:1, span]
            new = jnp.maximum(old, top)
            factor = jnp.exp(old - new)
            w0 = jnp.exp(masked[0] - new)
            w1 = jnp.exp(masked[1] - new)
            max_sc[0:1, span] = new
            tot_sc[0:1, span] = tot_sc[0:1, span] * factor + jnp.sum(
                w0 + w1, axis=0, keepdims=True
            )
            added = lax.dot_general(
                jnp.concatenate(aux, axis=1),
                jnp.concatenate([w0, w1], axis=0).astype(jnp.bfloat16),
                (((1,), (0,)), ((), ())),
                preferred_element_type=jnp.float32,
            )
            sum_sc[:, span] = sum_sc[:, span] * factor + added

    def step(s, carry):
        lo, hi = z - s, z + s
        has_lo, has_hi = lo >= 0, hi < depth
        lo_y, hi_y = z - s + 1, z + s - 1
        has_lo_y = lo_y >= 0
        has_hi_y = (hi_y < depth) & (s > 1)

        @pl.when(has_lo)
        def _():
            to_up(lo).wait_recv()

            @pl.when(has_up)
            def _():
                to_up(lo).start()

            to_y(lo).start()
            to_core(lo, y).start()

        @pl.when(has_hi & (s > 0))
        def _():
            to_dn(hi).wait_recv()

            @pl.when(has_dn)
            def _():
                to_dn(hi).start()

            to_y(hi).start()
            to_core(hi, y).start()

        @pl.when(has_lo_y)
        def _():
            from_y(lo_y).wait_recv()
            to_core(lo_y, 1 - y).start()

        @pl.when(has_hi_y)
        def _():
            from_y(hi_y).wait_recv()
            to_core(hi_y, 1 - y).start()

        def take(q, carry_q):
            side, late = q % 2, q // 2
            dist = s - late
            o = z + (2 * side - 1) * dist
            yy = y + late * (1 - 2 * y)

            @pl.when((o >= 0) & (o < depth) & ((dist > 0) | (side == 0)))
            def _():
                from_core(o, yy).wait_recv()
                absorb(o, yy)

            return carry_q

        return lax.fori_loop(0, 4, take, carry)

    from_core(z, y).wait_recv()
    absorb(z, y)
    lax.fori_loop(1, depth + 1, step, 0)

    def drain(o, carry):
        to_y(o).wait_send()
        to_core(o, 0).wait_send()
        to_core(o, 1).wait_send()

        @pl.when(has_up & (o <= z))
        def _():
            to_up(o).wait_send()

        @pl.when(has_dn & (o >= z))
        def _():
            to_dn(o).wait_send()

        return carry

    lax.fori_loop(0, depth, drain, 0)

    total = tot_sc[...]
    mean_ref[...] = sum_sc[0:nparam, :] / total
    lev = max_sc[...] + jnp.log(total)
    for i in range(rows // LANES):
        lanes = slice(i * LANES, (i + 1) * LANES)
        lev_ref[lanes] = lev[0:1, lanes].reshape(LANES)


def solution(mesh):
    depth = mesh.shape["blk"] // 4

    def on_device(observed, sharpness, obs_class, pattern, evolved, sim_params, sim_class):
        rows, feat = observed.shape
        sims = evolved.shape[0]
        nparam = sim_params.shape[0]
        packet_rows = feat // LANES * sims + AUX_ROWS
        vmem = pl.BlockSpec(memory_space=pltpu.VMEM)
        hbm = pl.BlockSpec(memory_space=pltpu.HBM)
        dma = pltpu.SemaphoreType.DMA
        mean, lev = pl.pallas_call(
            functools.partial(kernel, depth),
            out_shape=(
                jax.ShapeDtypeStruct((nparam, rows), jnp.float32),
                jax.ShapeDtypeStruct((rows,), jnp.float32),
            ),
            in_specs=[hbm] * 7,
            out_specs=(vmem, vmem),
            scratch_shapes=[
                pltpu.VMEM((depth, 2, 2, packet_rows, LANES), jnp.bfloat16),
                pltpu.VMEM((rows, feat), jnp.bfloat16),
                pltpu.VMEM((sims, feat), jnp.bfloat16),
                pltpu.VMEM((rows,), jnp.float32),
                pltpu.VMEM((rows,), jnp.int32),
                pltpu.SMEM(pattern.shape, jnp.int32),
                pltpu.VMEM((nparam, sims), jnp.bfloat16),
                pltpu.VMEM((sims,), jnp.int32),
                pltpu.VMEM((AUX_ROWS, LANES), jnp.float32),
                pltpu.VMEM((1, rows), jnp.float32),
                pltpu.VMEM((1, rows), jnp.int32),
                pltpu.VMEM((1, rows), jnp.float32),
                pltpu.VMEM((1, rows), jnp.float32),
                pltpu.VMEM((1, rows), jnp.float32),
                pltpu.VMEM((AUX_ROWS, rows), jnp.float32),
                dma((7,)),
                dma((depth,)),
                dma((depth,)),
                dma((depth,)),
                dma((2 * depth,)),
                dma((depth,)),
                dma((depth,)),
                dma((2 * depth,)),
            ],
            compiler_params=pltpu.CompilerParams(
                collective_id=0, has_side_effects=True, vmem_limit_bytes=60 << 20
            ),
        )(
            observed,
            sharpness,
            obs_class,
            pattern,
            evolved,
            sim_params,
            sim_class,
        )
        return mean, lev

    placed = (
        P(("parts", "blk"), None),
        P(("parts", "blk")),
        P(("parts", "blk")),
        P(("parts", "blk"), None),
        P(("parts", "blk"), None),
        P(None, ("parts", "blk")),
        P(("parts", "blk")),
    )
    return jax.shard_map(
        on_device,
        mesh=mesh,
        in_specs=placed,
        out_specs=(P(None, ("parts", "blk")), P(("parts", "blk"))),
        check_vma=False,
    )
```

```python
import functools

import jax
import jax.numpy as jnp
from jax import lax
from jax.experimental import pallas as pl
from jax.experimental.pallas import tpu as pltpu
from jax.sharding import PartitionSpec as P

NEG_START = -1e30
NEG_MASK = -3e38
LANES = 128
AUX_ROWS = 16
LATE = 2
MESH = pl.DeviceIdType.MESH


def kernel(
    depth,
    obs_hbm,
    sharp_hbm,
    ocls_hbm,
    pat_hbm,
    evo_hbm,
    prm_hbm,
    scls_hbm,
    mean_ref,
    lev_ref,
    gat,
    obs,
    evo,
    sharp_in,
    ocls_in,
    pat_ref,
    prm_ref,
    scls_in,
    stage,
    sharp_ref,
    ocls_ref,
    base_sc,
    max_sc,
    tot_sc,
    sum_sc,
    local_sem,
    up_send,
    dn_send,
    y_send,
    s_send,
    z_recv,
    y_recv,
    s_recv,
):
    me = lax.axis_index("blk")
    z, y, c = me // 4, (me // 2) % 2, me % 2
    rows, feat = obs.shape
    sims = evo.shape[0]
    tiles = feat // LANES
    tile_count = pat_hbm.shape[0]
    tile_rows = rows // tile_count
    nparam = prm_hbm.shape[0]

    def blk_of(zz, yy, cc):
        return zz * 4 + yy * 2 + cc

    evo_copy = pltpu.make_async_copy(evo_hbm, evo, local_sem.at[0])
    prm_copy = pltpu.make_async_copy(prm_hbm, prm_ref, local_sem.at[1])
    scls_copy = pltpu.make_async_copy(scls_hbm, scls_in, local_sem.at[2])
    obs_copy = pltpu.make_async_copy(obs_hbm, obs, local_sem.at[3])
    sharp_copy = pltpu.make_async_copy(sharp_hbm, sharp_in, local_sem.at[4])
    ocls_copy = pltpu.make_async_copy(ocls_hbm, ocls_in, local_sem.at[5])
    pat_copy = pltpu.make_async_copy(pat_hbm, pat_ref, local_sem.at[6])
    for copy in (evo_copy, prm_copy, scls_copy, obs_copy, sharp_copy, ocls_copy, pat_copy):
        copy.start()

    has_up = z < depth - 1
    has_dn = z > 0
    inner = ((z + depth - 1) // depth) * ((2 * depth - 2 - z) // depth)

    barrier = pltpu.get_barrier_semaphore()

    def greet(dev):
        pl.semaphore_signal(barrier, inc=1, device_id={"blk": dev}, device_id_type=MESH)

    greet(blk_of(z, y, 1 - c))
    greet(blk_of(z, 1 - y, c))

    @pl.when(has_up)
    def _():
        greet(blk_of(z + 1, y, c))

    @pl.when(has_dn)
    def _():
        greet(blk_of(z - 1, y, c))

    stage[...] = jnp.zeros_like(stage)
    prm_copy.wait()
    stage[0:nparam, :] = prm_ref[...].astype(jnp.float32)
    scls_copy.wait()
    stage[nparam : nparam + 1, :] = scls_in[...].reshape(1, sims).astype(jnp.float32)
    evo_copy.wait()
    for t in range(tiles):
        gat[z, y, c, t * sims : (t + 1) * sims, :] = evo[:, t * LANES : (t + 1) * LANES]
    gat[z, y, c, tiles * sims : tiles * sims + AUX_ROWS, :] = stage[...].astype(jnp.bfloat16)

    peers = 2 + (z + depth - 1) // depth + (2 * depth - 2 - z) // depth
    pl.semaphore_wait(barrier, peers)

    total_rows = gat.shape[3]
    early = (total_rows + 95) // 96 * 16
    cuts = [early + (total_rows - early) * k // (16 * LATE) * 16 for k in range(LATE)] + [total_rows]
    pieces = [(cuts[k], cuts[k + 1] - cuts[k]) for k in range(LATE)] + [(0, early)]

    def hop(o, yy, k, dev, send, recv):
        ref = gat.at[o, yy, c, pl.ds(*pieces[k])]
        return pltpu.make_async_remote_copy(
            src_ref=ref,
            dst_ref=ref,
            send_sem=send,
            recv_sem=recv,
            device_id={"blk": dev},
            device_id_type=MESH,
        )

    def along_z(o, j, zz, send):
        yy, k = (y, j) if j <= LATE else (1 - y, LATE)
        slot = o * (LATE + 2) + j
        return hop(o, yy, k, blk_of(zz, y, c), send.at[slot], z_recv.at[slot])

    def to_up(o, j):
        return along_z(o, j, z + 1, up_send)

    def to_dn(o, j):
        return along_z(o, j, z - 1, dn_send)

    def across_y(o, yy, k):
        slot = o * (LATE + 1) + k
        return hop(o, yy, k, blk_of(z, 1 - y, c), y_send.at[slot], y_recv.at[slot])

    def to_y(o, k):
        return across_y(o, y, k)

    def from_y(o, k):
        return across_y(o, 1 - y, k)

    def core_hop(o, yy, cc, part):
        span = pl.ds(0, early) if part else pl.ds(early, total_rows - early)
        ref = gat.at[o, yy, cc, span]
        slot = (o * 2 + yy) * 2 + part
        return pltpu.make_async_remote_copy(
            src_ref=ref,
            dst_ref=ref,
            send_sem=s_send.at[slot],
            recv_sem=s_recv.at[slot],
            device_id={"blk": blk_of(z, y, 1 - c)},
            device_id_type=MESH,
        )

    def to_core(o, yy, part):
        return core_hop(o, yy, c, part)

    def from_core(o, yy, part):
        return core_hop(o, yy, 1 - c, part)

    def own_both_ways(j):
        @pl.when(has_up)
        def _():
            to_up(z, j).start()

        @pl.when(has_dn)
        def _():
            to_dn(z, j).start()

    to_y(z, LATE).start()
    for j in range(LATE):
        own_both_ways(j)
        to_y(z, j).start()
    to_core(z, y, 0).start()
    to_core(z, y, 1).start()

    sharp_copy.wait()
    ocls_copy.wait()
    pat_copy.wait()
    obs_copy.wait()
    for i in range(rows // LANES):
        lanes = slice(i * LANES, (i + 1) * LANES)
        sharp_ref[0:1, lanes] = 2.0 * sharp_in[lanes].reshape(1, LANES)
        ocls_ref[0:1, lanes] = ocls_in[lanes].reshape(1, LANES)
        part = obs[i * LANES : (i + 1) * LANES, :].astype(jnp.float32)
        col = jnp.sum(part * part, axis=1, keepdims=True)
        wide = jnp.broadcast_to(col, (LANES, LANES)).T
        base_sc[0:1, i * LANES : (i + 1) * LANES] = 1.0 * feat - 0.5 * wide[0:1, :]

    max_sc[...] = jnp.full_like(max_sc, NEG_START)
    tot_sc[...] = jnp.zeros_like(tot_sc)
    sum_sc[...] = jnp.zeros_like(sum_sc)
    group = 2 if tile_count % 2 == 0 else 1
    width = group * tile_rows

    def absorb(o, yy):
        lhs, half_sq, classes, aux = [], [], [], []
        for cc in range(2):
            block = jnp.concatenate(
                [gat[o, yy, cc, t * sims : (t + 1) * sims, :] for t in range(tiles)], axis=1
            )
            wide = block.astype(jnp.float32)
            half_sq.append(0.5 * jnp.sum(wide * wide, axis=1, keepdims=True))
            extra = gat[o, yy, cc, tiles * sims : tiles * sims + AUX_ROWS, :]
            row = extra.astype(jnp.float32)[nparam : nparam + 1, :]
            turned = jnp.broadcast_to(row, (LANES, LANES)).T
            classes.append(turned[:, 0:1])
            aux.append(extra)
            lhs.append(block)
        lhs = jnp.concatenate(lhs, axis=0)
        for g in range(tile_count // group):
            span = slice(g * width, (g + 1) * width)
            product = lax.dot_general(
                lhs, obs[span, :], (((1,), (1,)), ((), ())), preferred_element_type=jnp.float32
            )
            sharp2 = sharp_ref[0:1, span]
            base = base_sc[0:1, span]
            masked = []
            for cc in range(2):
                wanted = jnp.concatenate(
                    [
                        jnp.where(
                            pat_ref[i, blk_of(o, yy, cc)] == 1,
                            ocls_ref[0:1, i * tile_rows : (i + 1) * tile_rows],
                            -1,
                        )
                        for i in range(g * group, (g + 1) * group)
                    ],
                    axis=1,
                ).astype(jnp.float32)
                score = ((product[cc * sims : (cc + 1) * sims] - half_sq[cc]) + base) * sharp2
                masked.append(jnp.where(classes[cc] == wanted, score, NEG_MASK))
            top = jnp.max(jnp.maximum(masked[0], masked[1]), axis=0, keepdims=True)
            old = max_sc[0:1, span]
            new = jnp.maximum(old, top)
            factor = jnp.exp(old - new)
            w0 = jnp.exp(masked[0] - new)
            w1 = jnp.exp(masked[1] - new)
            max_sc[0:1, span] = new
            tot_sc[0:1, span] = tot_sc[0:1, span] * factor + jnp.sum(
                w0 + w1, axis=0, keepdims=True
            )
            added = lax.dot_general(
                jnp.concatenate(aux, axis=1),
                jnp.concatenate([w0, w1], axis=0).astype(jnp.bfloat16),
                (((1,), (0,)), ((), ())),
                preferred_element_type=jnp.float32,
            )
            sum_sc[:, span] = sum_sc[:, span] * factor + added

    def step(s, carry):
        def sides(dist):
            lo, hi = z - dist, z + dist
            return ((lo, lo >= 0, has_up, to_up), (hi, (hi < depth) & (dist > 0), has_dn, to_dn))

        for j in range(LATE):
            for o, there, further, to in sides(s):

                @pl.when(there)
                def _():
                    to(o, j).wait_recv()

                    @pl.when(further)
                    def _():
                        to(o, j).start()

                    to_y(o, j).start()
                    if j == LATE - 1:
                        to_core(o, y, 0).start()

        @pl.when(s == 1)
        def _():
            own_both_ways(LATE)
            from_y(z, LATE).wait_recv()
            own_both_ways(LATE + 1)
            to_core(z, 1 - y, 1).start()

        for j, yy in ((LATE, y), (LATE + 1, 1 - y)):
            for o, there, further, to in sides(s - 1):

                @pl.when(there & (s > 1))
                def _():
                    to(o, j).wait_recv()

                    @pl.when(further)
                    def _():
                        to(o, j).start()

                    to_core(o, yy, 1).start()

        done = s - 1 - inner

        for o, there, further, to in sides(done):

            @pl.when(there & (done >= 0))
            def _():
                for k in range(LATE):
                    from_y(o, k).wait_recv()
                to_core(o, 1 - y, 0).start()

        def pick(q, carry_q):
            side, other = q % 2, q // 2
            o = z + (2 * side - 1) * done
            yy = y + other * (1 - 2 * y)

            @pl.when((o >= 0) & (o < depth) & (done >= 0) & ((done > 0) | (side == 0)))
            def _():
                from_core(o, yy, 0).wait_recv()
                from_core(o, yy, 1).wait_recv()
                absorb(o, yy)

            return carry_q

        return lax.fori_loop(0, 4, pick, carry)

    lax.fori_loop(1, depth + 1, step, 0)

    def drain(o, carry):
        for part in range(2):
            to_core(o, 0, part).wait_send()
            to_core(o, 1, part).wait_send()
        for k in range(LATE):
            to_y(o, k).wait_send()
        for j in range(LATE + 2):

            @pl.when(has_up & (o <= z))
            def _():
                to_up(o, j).wait_send()

            @pl.when(has_dn & (o >= z))
            def _():
                to_dn(o, j).wait_send()

        return carry

    to_y(z, LATE).wait_send()
    lax.fori_loop(0, depth, drain, 0)

    total = tot_sc[...]
    mean_ref[...] = sum_sc[0:nparam, :] / total
    lev = max_sc[...] + jnp.log(total)
    for i in range(rows // LANES):
        lanes = slice(i * LANES, (i + 1) * LANES)
        lev_ref[lanes] = lev[0:1, lanes].reshape(LANES)


def solution(mesh):
    depth = mesh.shape["blk"] // 4

    def on_device(observed, sharpness, obs_class, pattern, evolved, sim_params, sim_class):
        rows, feat = observed.shape
        sims = evolved.shape[0]
        nparam = sim_params.shape[0]
        packet_rows = feat // LANES * sims + AUX_ROWS
        vmem = pl.BlockSpec(memory_space=pltpu.VMEM)
        hbm = pl.BlockSpec(memory_space=pltpu.HBM)
        dma = pltpu.SemaphoreType.DMA
        mean, lev = pl.pallas_call(
            functools.partial(kernel, depth),
            out_shape=(
                jax.ShapeDtypeStruct((nparam, rows), jnp.float32),
                jax.ShapeDtypeStruct((rows,), jnp.float32),
            ),
            in_specs=[hbm] * 7,
            out_specs=(vmem, vmem),
            scratch_shapes=[
                pltpu.VMEM((depth, 2, 2, packet_rows, LANES), jnp.bfloat16),
                pltpu.VMEM((rows, feat), jnp.bfloat16),
                pltpu.VMEM((sims, feat), jnp.bfloat16),
                pltpu.VMEM((rows,), jnp.float32),
                pltpu.VMEM((rows,), jnp.int32),
                pltpu.SMEM(pattern.shape, jnp.int32),
                pltpu.VMEM((nparam, sims), jnp.bfloat16),
                pltpu.VMEM((sims,), jnp.int32),
                pltpu.VMEM((AUX_ROWS, LANES), jnp.float32),
                pltpu.VMEM((1, rows), jnp.float32),
                pltpu.VMEM((1, rows), jnp.int32),
                pltpu.VMEM((1, rows), jnp.float32),
                pltpu.VMEM((1, rows), jnp.float32),
                pltpu.VMEM((1, rows), jnp.float32),
                pltpu.VMEM((AUX_ROWS, rows), jnp.float32),
                dma((7,)),
                dma(((LATE + 2) * depth,)),
                dma(((LATE + 2) * depth,)),
                dma(((LATE + 1) * depth,)),
                dma((4 * depth,)),
                dma(((LATE + 2) * depth,)),
                dma(((LATE + 1) * depth,)),
                dma((4 * depth,)),
            ],
            compiler_params=pltpu.CompilerParams(
                collective_id=0, has_side_effects=True, vmem_limit_bytes=60 << 20
            ),
        )(
            observed,
            sharpness,
            obs_class,
            pattern,
            evolved,
            sim_params,
            sim_class,
        )
        return mean, lev

    placed = (
        P(("parts", "blk"), None),
        P(("parts", "blk")),
        P(("parts", "blk")),
        P(("parts", "blk"), None),
        P(("parts", "blk"), None),
        P(None, ("parts", "blk")),
        P(("parts", "blk")),
    )
    return jax.shard_map(
        on_device,
        mesh=mesh,
        in_specs=placed,
        out_specs=(P(None, ("parts", "blk")), P(("parts", "blk"))),
        check_vma=False,
    )
```

```python
import functools

import jax
import jax.numpy as jnp
from jax import lax
from jax.experimental import pallas as pl
from jax.experimental.pallas import tpu as pltpu
from jax.sharding import PartitionSpec as P

NEG_START = -1e30
NEG_MASK = -3e38
LANES = 128
AUX_ROWS = 16
LATE = 3
MESH = pl.DeviceIdType.MESH


def kernel(
    depth,
    obs_hbm,
    sharp_hbm,
    ocls_hbm,
    pat_hbm,
    evo_hbm,
    prm_hbm,
    scls_hbm,
    mean_ref,
    lev_ref,
    gat,
    obs,
    evo,
    sharp_in,
    ocls_in,
    pat_ref,
    prm_ref,
    scls_in,
    stage,
    sharp_ref,
    ocls_ref,
    base_sc,
    max_sc,
    tot_sc,
    sum_sc,
    local_sem,
    up_send,
    dn_send,
    y_send,
    s_send,
    z_recv,
    y_recv,
    s_recv,
):
    me = lax.axis_index("blk")
    z, y, c = me // 4, (me // 2) % 2, me % 2
    rows, feat = obs.shape
    sims = evo.shape[0]
    tiles = feat // LANES
    tile_count = pat_hbm.shape[0]
    tile_rows = rows // tile_count
    nparam = prm_hbm.shape[0]

    def blk_of(zz, yy, cc):
        return zz * 4 + yy * 2 + cc

    evo_copy = pltpu.make_async_copy(evo_hbm, evo, local_sem.at[0])
    prm_copy = pltpu.make_async_copy(prm_hbm, prm_ref, local_sem.at[1])
    scls_copy = pltpu.make_async_copy(scls_hbm, scls_in, local_sem.at[2])
    obs_copy = pltpu.make_async_copy(obs_hbm, obs, local_sem.at[3])
    sharp_copy = pltpu.make_async_copy(sharp_hbm, sharp_in, local_sem.at[4])
    ocls_copy = pltpu.make_async_copy(ocls_hbm, ocls_in, local_sem.at[5])
    pat_copy = pltpu.make_async_copy(pat_hbm, pat_ref, local_sem.at[6])
    for copy in (evo_copy, prm_copy, scls_copy, obs_copy, sharp_copy, ocls_copy, pat_copy):
        copy.start()

    has_up = z < depth - 1
    has_dn = z > 0
    inner = ((z + depth - 1) // depth) * ((2 * depth - 2 - z) // depth)

    barrier = pltpu.get_barrier_semaphore()

    def greet(dev):
        pl.semaphore_signal(barrier, inc=1, device_id={"blk": dev}, device_id_type=MESH)

    greet(blk_of(z, y, 1 - c))
    greet(blk_of(z, 1 - y, c))

    @pl.when(has_up)
    def _():
        greet(blk_of(z + 1, y, c))

    @pl.when(has_dn)
    def _():
        greet(blk_of(z - 1, y, c))

    stage[...] = jnp.zeros_like(stage)
    prm_copy.wait()
    stage[0:nparam, :] = prm_ref[...].astype(jnp.float32)
    scls_copy.wait()
    stage[nparam : nparam + 1, :] = scls_in[...].reshape(1, sims).astype(jnp.float32)
    evo_copy.wait()
    own = evo[...].astype(jnp.float32)
    own_sq = 0.5 * jnp.sum(own * own, axis=1, keepdims=True)
    left = jnp.broadcast_to(own_sq, (LANES, LANES)).T[0:1, :]
    for k in range(3):
        part = left.astype(jnp.bfloat16).astype(jnp.float32)
        stage[nparam + 1 + k : nparam + 2 + k, :] = part
        left = left - part
    for t in range(tiles):
        gat[z, y, c, t * sims : (t + 1) * sims, :] = evo[:, t * LANES : (t + 1) * LANES]
    gat[z, y, c, tiles * sims : tiles * sims + AUX_ROWS, :] = stage[...].astype(jnp.bfloat16)

    peers = 2 + (z + depth - 1) // depth + (2 * depth - 2 - z) // depth
    pl.semaphore_wait(barrier, peers)

    total_rows = gat.shape[3]
    early = (total_rows + 95) // 96 * 16
    cuts = [early + (total_rows - early) * k // (16 * LATE) * 16 for k in range(LATE)] + [total_rows]
    pieces = [(cuts[k], cuts[k + 1] - cuts[k]) for k in range(LATE)] + [(0, early)]

    def hop(o, yy, k, dev, send, recv):
        ref = gat.at[o, yy, c, pl.ds(*pieces[k])]
        return pltpu.make_async_remote_copy(
            src_ref=ref,
            dst_ref=ref,
            send_sem=send,
            recv_sem=recv,
            device_id={"blk": dev},
            device_id_type=MESH,
        )

    def along_z(o, j, zz, send):
        yy, k = (y, j) if j <= LATE else (1 - y, LATE)
        slot = o * (LATE + 2) + j
        return hop(o, yy, k, blk_of(zz, y, c), send.at[slot], z_recv.at[slot])

    def to_up(o, j):
        return along_z(o, j, z + 1, up_send)

    def to_dn(o, j):
        return along_z(o, j, z - 1, dn_send)

    def across_y(o, yy, k):
        slot = o * (LATE + 1) + k
        return hop(o, yy, k, blk_of(z, 1 - y, c), y_send.at[slot], y_recv.at[slot])

    def to_y(o, k):
        return across_y(o, y, k)

    def from_y(o, k):
        return across_y(o, 1 - y, k)

    def core_hop(o, yy, cc, part):
        span = pl.ds(0, early) if part else pl.ds(early, total_rows - early)
        ref = gat.at[o, yy, cc, span]
        slot = (o * 2 + yy) * 2 + part
        return pltpu.make_async_remote_copy(
            src_ref=ref,
            dst_ref=ref,
            send_sem=s_send.at[slot],
            recv_sem=s_recv.at[slot],
            device_id={"blk": blk_of(z, y, 1 - c)},
            device_id_type=MESH,
        )

    def to_core(o, yy, part):
        return core_hop(o, yy, c, part)

    def from_core(o, yy, part):
        return core_hop(o, yy, 1 - c, part)

    def own_both_ways(j):
        @pl.when(has_up)
        def _():
            to_up(z, j).start()

        @pl.when(has_dn)
        def _():
            to_dn(z, j).start()

    to_y(z, LATE).start()
    for j in range(LATE):
        own_both_ways(j)
        to_y(z, j).start()
    to_core(z, y, 0).start()
    to_core(z, y, 1).start()

    sharp_copy.wait()
    ocls_copy.wait()
    pat_copy.wait()
    obs_copy.wait()
    for i in range(rows // LANES):
        lanes = slice(i * LANES, (i + 1) * LANES)
        sharp_ref[0:1, lanes] = 2.0 * sharp_in[lanes].reshape(1, LANES)
        ocls_ref[0:1, lanes] = ocls_in[lanes].reshape(1, LANES)
        part = obs[i * LANES : (i + 1) * LANES, :].astype(jnp.float32)
        col = jnp.sum(part * part, axis=1, keepdims=True)
        wide = jnp.broadcast_to(col, (LANES, LANES)).T
        base_sc[0:1, i * LANES : (i + 1) * LANES] = 1.0 * feat - 0.5 * wide[0:1, :]

    max_sc[...] = jnp.full_like(max_sc, NEG_START)
    tot_sc[...] = jnp.zeros_like(tot_sc)
    sum_sc[...] = jnp.zeros_like(sum_sc)
    group = tile_count
    width = group * tile_rows

    def absorb(o, yy):
        lhs, half_sq, classes, aux = [], [], [], []
        for cc in range(2):
            block = jnp.concatenate(
                [gat[o, yy, cc, t * sims : (t + 1) * sims, :] for t in range(tiles)], axis=1
            )
            extra = gat[o, yy, cc, tiles * sims : tiles * sims + AUX_ROWS, :]
            rows_f32 = extra.astype(jnp.float32)
            row = rows_f32[nparam : nparam + 1, :]
            row_sq = (
                rows_f32[nparam + 1 : nparam + 2, :]
                + rows_f32[nparam + 2 : nparam + 3, :]
                + rows_f32[nparam + 3 : nparam + 4, :]
            )
            classes.append(jnp.broadcast_to(row, (LANES, LANES)).T[:, 0:1])
            half_sq.append(jnp.broadcast_to(row_sq, (LANES, LANES)).T[:, 0:1])
            aux.append(extra)
            lhs.append(block)
        lhs = jnp.concatenate(lhs, axis=0)
        for g in range(tile_count // group):
            span = slice(g * width, (g + 1) * width)
            product = lax.dot_general(
                lhs, obs[span, :], (((1,), (1,)), ((), ())), preferred_element_type=jnp.float32
            )
            sharp2 = sharp_ref[0:1, span]
            base = base_sc[0:1, span]
            masked = []
            for cc in range(2):
                wanted = jnp.concatenate(
                    [
                        jnp.where(
                            pat_ref[i, blk_of(o, yy, cc)] == 1,
                            ocls_ref[0:1, i * tile_rows : (i + 1) * tile_rows],
                            -1,
                        )
                        for i in range(g * group, (g + 1) * group)
                    ],
                    axis=1,
                ).astype(jnp.float32)
                score = ((product[cc * sims : (cc + 1) * sims] - half_sq[cc]) + base) * sharp2
                masked.append(jnp.where(classes[cc] == wanted, score, NEG_MASK))
            top = jnp.max(jnp.maximum(masked[0], masked[1]), axis=0, keepdims=True)
            old = max_sc[0:1, span]
            new = jnp.maximum(old, top)
            factor = jnp.exp(old - new)
            w0 = jnp.exp(masked[0] - new)
            w1 = jnp.exp(masked[1] - new)
            max_sc[0:1, span] = new
            tot_sc[0:1, span] = tot_sc[0:1, span] * factor + jnp.sum(
                w0 + w1, axis=0, keepdims=True
            )
            added = lax.dot_general(
                jnp.concatenate(aux, axis=1),
                jnp.concatenate([w0, w1], axis=0).astype(jnp.bfloat16),
                (((1,), (0,)), ((), ())),
                preferred_element_type=jnp.float32,
            )
            sum_sc[:, span] = sum_sc[:, span] * factor + added

    def step(s, carry):
        def sides(dist):
            lo, hi = z - dist, z + dist
            return ((lo, lo >= 0, has_up, to_up), (hi, (hi < depth) & (dist > 0), has_dn, to_dn))

        for j in range(LATE):
            for o, there, further, to in sides(s):

                @pl.when(there)
                def _():
                    to(o, j).wait_recv()

                    @pl.when(further)
                    def _():
                        to(o, j).start()

                    to_y(o, j).start()
                    if j == LATE - 1:
                        to_core(o, y, 0).start()

        @pl.when(s == 1)
        def _():
            own_both_ways(LATE)
            from_y(z, LATE).wait_recv()
            own_both_ways(LATE + 1)
            to_core(z, 1 - y, 1).start()

        for j, yy in ((LATE, y), (LATE + 1, 1 - y)):
            for o, there, further, to in sides(s - 1):

                @pl.when(there & (s > 1))
                def _():
                    to(o, j).wait_recv()

                    @pl.when(further)
                    def _():
                        to(o, j).start()

                    to_core(o, yy, 1).start()

        done = s - 1 - inner

        for o, there, further, to in sides(done):

            @pl.when(there & (done >= 0))
            def _():
                for k in range(LATE):
                    from_y(o, k).wait_recv()
                to_core(o, 1 - y, 0).start()

        def pick(q, carry_q):
            side, other = q % 2, q // 2
            o = z + (2 * side - 1) * done
            yy = y + other * (1 - 2 * y)

            @pl.when((o >= 0) & (o < depth) & (done >= 0) & ((done > 0) | (side == 0)))
            def _():
                from_core(o, yy, 0).wait_recv()
                from_core(o, yy, 1).wait_recv()
                absorb(o, yy)

            return carry_q

        return lax.fori_loop(0, 4, pick, carry)

    lax.fori_loop(1, depth + 1, step, 0)

    def drain(o, carry):
        for part in range(2):
            to_core(o, 0, part).wait_send()
            to_core(o, 1, part).wait_send()
        for k in range(LATE):
            to_y(o, k).wait_send()
        for j in range(LATE + 2):

            @pl.when(has_up & (o <= z))
            def _():
                to_up(o, j).wait_send()

            @pl.when(has_dn & (o >= z))
            def _():
                to_dn(o, j).wait_send()

        return carry

    to_y(z, LATE).wait_send()
    lax.fori_loop(0, depth, drain, 0)

    total = tot_sc[...]
    mean_ref[...] = sum_sc[0:nparam, :] / total
    lev = max_sc[...] + jnp.log(total)
    for i in range(rows // LANES):
        lanes = slice(i * LANES, (i + 1) * LANES)
        lev_ref[lanes] = lev[0:1, lanes].reshape(LANES)


def solution(mesh):
    depth = mesh.shape["blk"] // 4

    def on_device(observed, sharpness, obs_class, pattern, evolved, sim_params, sim_class):
        rows, feat = observed.shape
        sims = evolved.shape[0]
        nparam = sim_params.shape[0]
        packet_rows = feat // LANES * sims + AUX_ROWS
        vmem = pl.BlockSpec(memory_space=pltpu.VMEM)
        hbm = pl.BlockSpec(memory_space=pltpu.HBM)
        dma = pltpu.SemaphoreType.DMA
        mean, lev = pl.pallas_call(
            functools.partial(kernel, depth),
            out_shape=(
                jax.ShapeDtypeStruct((nparam, rows), jnp.float32),
                jax.ShapeDtypeStruct((rows,), jnp.float32),
            ),
            in_specs=[hbm] * 7,
            out_specs=(vmem, vmem),
            scratch_shapes=[
                pltpu.VMEM((depth, 2, 2, packet_rows, LANES), jnp.bfloat16),
                pltpu.VMEM((rows, feat), jnp.bfloat16),
                pltpu.VMEM((sims, feat), jnp.bfloat16),
                pltpu.VMEM((rows,), jnp.float32),
                pltpu.VMEM((rows,), jnp.int32),
                pltpu.SMEM(pattern.shape, jnp.int32),
                pltpu.VMEM((nparam, sims), jnp.bfloat16),
                pltpu.VMEM((sims,), jnp.int32),
                pltpu.VMEM((AUX_ROWS, LANES), jnp.float32),
                pltpu.VMEM((1, rows), jnp.float32),
                pltpu.VMEM((1, rows), jnp.int32),
                pltpu.VMEM((1, rows), jnp.float32),
                pltpu.VMEM((1, rows), jnp.float32),
                pltpu.VMEM((1, rows), jnp.float32),
                pltpu.VMEM((AUX_ROWS, rows), jnp.float32),
                dma((7,)),
                dma(((LATE + 2) * depth,)),
                dma(((LATE + 2) * depth,)),
                dma(((LATE + 1) * depth,)),
                dma((4 * depth,)),
                dma(((LATE + 2) * depth,)),
                dma(((LATE + 1) * depth,)),
                dma((4 * depth,)),
            ],
            compiler_params=pltpu.CompilerParams(
                collective_id=0, has_side_effects=True, vmem_limit_bytes=60 << 20
            ),
        )(
            observed,
            sharpness,
            obs_class,
            pattern,
            evolved,
            sim_params,
            sim_class,
        )
        return mean, lev

    placed = (
        P(("parts", "blk"), None),
        P(("parts", "blk")),
        P(("parts", "blk")),
        P(("parts", "blk"), None),
        P(("parts", "blk"), None),
        P(None, ("parts", "blk")),
        P(("parts", "blk")),
    )
    return jax.shard_map(
        on_device,
        mesh=mesh,
        in_specs=placed,
        out_specs=(P(None, ("parts", "blk")), P(("parts", "blk"))),
        check_vma=False,
    )
```
